32 devices in a mesh: grp: 2 (over core), dev: 16 (over z, y, x).
Axes of the slice: x: 2, y: 2, z: 4, core: 2. Of those that a mesh axis runs over, the one named last changes fastest.
Arguments:
- tokens: bfloat16 [8192, 2048], P(('grp', 'dev')), may hold values from -6 to 6
- modulation: float32 [32, 12288], P(('grp', 'dev')), may hold values from -3 to 3
- w_query: bfloat16 [2048, 1024], P(('grp', 'dev')), may hold values from -1 to 1
- w_key: bfloat16 [2048, 1024], P(('grp', 'dev')), may hold values from -1 to 1
- w_value: bfloat16 [2048, 1024], P(('grp', 'dev')), may hold values from -0.125 to 0.125
- w_out: bfloat16 [1024, 2048], P(None, ('grp', 'dev')), may hold values from -0.1875 to 0.1875
- w_in: bfloat16 [16, 2048, 4096], P('dev', None, 'grp'), may hold values from -0.125 to 0.125
- w_back: bfloat16 [16, 4096, 2048], P('dev', 'grp'), may hold values from -0.09375 to 0.09375
- routes: int32 [8192, 2], P(('grp', 'dev')), may hold values from 0 to 15, all different within a row; in each aligned block of 256 rows (0 to 255, 256 to 511, ...) at most 40 rows name the same one
- route_prob: float32 [8192, 2], P(('grp', 'dev')), may hold values from 0.2 to 1
Outputs:
- block_out: bfloat16 [8192, 2048], P(('grp', 'dev'))
The draws below stay inside these ranges and needn't reach their ends.
Inputs may be any that keep to these rules, and one draw needn't show every extreme that they name: `routes`: the 2 experts of a token differ. Among the 256 tokens of one device (aligned blocks of rows), no expert is named more than 40 times, a bound that some block reaches.
All inputs are finite; a program needn't handle non-finite values.
Results may differ from the reference program's by a relative error of at most 0.0055.
Values may be sent and summed in bfloat16 or wider, within the bound.
A program may use at most 128 MiB of HBM per device.

```python
import math
import jax
import jax.numpy as jnp
import numpy as np
from jax import lax

D = 2048
HEADS = 8
HDIM = 128
HW = 1024
HID = 4096
TOP = 2
E = 16
SEQ = 256
TOK_DEV = 256
IMAGES = 32
TOKENS = 8192
CAP = 40
N_GRP = 2
N_DEV = 16


def paired_query(key):
    base_rows = jnp.clip(jax.random.normal(jax.random.fold_in(key, 101), (D, HW), jnp.float32), -4.0, 4.0) * D ** (-0.5)
    noise_rows = jnp.clip(jax.random.normal(jax.random.fold_in(key, 202), (D, HW), jnp.float32), -4.0, 4.0) * D ** (-0.5)
    query_part = base_rows
    key_part = noise_rows
    return (jnp.clip(query_part, -1.0, 1.0), jnp.clip(key_part, -1.0, 1.0))


def draw_w_query(key, part):
    return paired_query(key)[0].astype(jnp.bfloat16)


def draw_w_key(key, part):
    return paired_query(key)[1].astype(jnp.bfloat16)


def level_of(key, dims, pieces, least, largest):
    loudness = 1.0
    for axis_at, shards_of in pieces:
        steps = jax.random.uniform(jax.random.fold_in(jax.random.fold_in(key, 6), axis_at), (shards_of,), jnp.float32, least / len(pieces), largest / len(pieces))
        loudness = loudness * jnp.repeat(jnp.exp(steps), dims[axis_at] // shards_of).reshape((-1,) + (1,) * (len(dims) - 1 - axis_at))
    return loudness


def shared_out(own_key, own, number, rows, amount, top, limit, skew):
    order = jax.random.permutation(own_key, amount)
    packed, common = shares(amount, rows * top, limit, skew, True), shares(amount, rows * top, limit, skew, False)
    places = jnp.arange(amount)

    def named(sizes, offset_by):
        used = int((sizes > 0).sum())
        fixed = max(1, used // 4)
        moved = fixed + (places - fixed + offset_by * (used - fixed)) % max(1, amount - fixed)
        return jnp.zeros((amount,), jnp.int32).at[order[jnp.where(places < fixed, places, moved)]].set(jnp.asarray(sizes, jnp.int32))

    sizes = jnp.where(number % 4 == 0, named(packed, number // 4), named(common, number - number // 4 - 1))
    mixed = jax.random.permutation(jax.random.fold_in(own, 3), amount)
    donor, taker = mixed[0:amount // 2 * 2:2], mixed[1:amount // 2 * 2:2]
    room = jnp.minimum(sizes[donor] - 1, limit - sizes[taker]) // 2
    room = jnp.where((donor == order[0]) | (taker == order[0]) | (sizes[taker] == 0), 0, jnp.maximum(room, 0))
    moved = jax.random.randint(jax.random.fold_in(own, 4), (amount // 2,), 0, 1 << 20) % (room + 1)
    sizes = sizes.at[donor].add(-moved).at[taker].add(moved)
    members = jnp.searchsorted(jnp.cumsum(sizes), jnp.arange(rows * top), side="right").astype(jnp.int32)
    table = members.reshape(top, rows).T
    table = table[jax.random.permutation(jax.random.fold_in(own, 1), rows)]
    offset_by = jax.random.randint(jax.random.fold_in(own, 2), (rows, 1), 0, top)
    return jnp.take_along_axis(table, (jnp.arange(top)[None, :] + offset_by) % top, axis=1)


def shares(count, total, most, skew, full):
    portions = [(1 << 20) // math.isqrt(rank ** skew) + 1 for rank in range(1, count + 1)]
    largest = most if full else min(most, max(-(-total // count), total * portions[0] // sum(portions)))
    least = 1 if total - largest >= count - 1 else 0
    given, rest = [largest] + [least] * (count - 1), total - largest - least * (count - 1)
    while rest > 0:
        free = [i for i in range(1, count) if given[i] < largest] or [i for i in range(1, count) if given[i] < most]
        pool, left = sum([portions[i] for i in free]), rest
        for i in free:
            addition = min(most - given[i], max(1, left * portions[i] // pool), rest)
            given[i] = given[i] + addition
            rest = rest - addition
    return np.array(given)


def noise(own_key, shape, scale, most, cuts=(), kind=jnp.bfloat16):
    loudness = level_of(own_key, shape, cuts, -0.22, 0.18) if cuts else 1.0
    drawn = jax.random.normal(own_key, shape, jnp.float32) * scale * loudness
    return jnp.minimum(jnp.maximum(drawn, -most), most).astype(kind)


def setup_inputs(seed: int = 0) -> dict:
    keys = jax.random.split(jax.random.key(seed), 11)
    tokens = noise(keys[0], (TOKENS, D), 1.0, 6.0, ((0, 32),))
    modulation = noise(keys[1], (IMAGES, 6 * D), 0.5, 3.0, ((0, 32),), jnp.float32)
    w_query = draw_w_query(jax.random.fold_in(keys[10], 71), 0)
    w_key = draw_w_key(jax.random.fold_in(keys[10], 71), 0)
    w_value = noise(keys[4], (D, HW), D ** -0.5, 0.125, ((0, 32),))
    w_out = noise(keys[5], (HW, D), HW ** -0.5, 0.1875, ((1, 32),))
    w_in = noise(keys[6], (E, D, HID), D ** -0.5, 0.125, ((0, 16), (2, 2)))
    w_back = noise(keys[7], (E, HID, D), HID ** -0.5, 0.09375, ((0, 16), (1, 2)))
    routes_keys = jax.random.split(jax.random.fold_in(keys[8], 1), TOKENS // TOK_DEV)
    routes_turns = jax.random.permutation(jax.random.fold_in(keys[8], 3), TOKENS // TOK_DEV)
    routes = jax.vmap(lambda own, number: shared_out(jax.random.fold_in(keys[8], 2), own, number, TOK_DEV, E, TOP, CAP, 2))(routes_keys, routes_turns).reshape((TOKENS, TOP))
    route_prob = jnp.clip(0.2 + 0.8 * jax.random.uniform(keys[9], (TOKENS, TOP), jnp.float32) ** level_of(keys[9], (TOKENS, TOP), ((0, 32),), -0.2, 0.2), 0.2, 1.0)
    return dict(tokens=tokens, modulation=modulation, w_query=w_query, w_key=w_key, w_value=w_value, w_out=w_out, w_in=w_in, w_back=w_back, routes=routes, route_prob=route_prob)


def normalize(values):
    row_mean = lax.optimization_barrier(jnp.mean(values, axis=-1, keepdims=True))
    centered = values - row_mean
    variance = lax.optimization_barrier(jnp.mean(centered * centered, axis=-1, keepdims=True))
    return centered * lax.rsqrt(variance + 1e-06)

def slot_table(choice_ids):
    onehot = (choice_ids[:, None] == jnp.arange(E, dtype=jnp.int32)[None, :]).astype(jnp.int32)
    before = jnp.cumsum(onehot, axis=0) - onehot
    return (choice_ids * CAP + lax.optimization_barrier(jnp.sum(before * onehot, axis=1))).astype(jnp.int32)

def reference(tokens, modulation, w_query, w_key, w_value, w_out, w_in, w_back, routes, route_prob):
    devices = N_GRP * N_DEV
    mod_terms = modulation.reshape(IMAGES, 6, 1, D)
    residual = tokens.astype(jnp.float32).reshape(IMAGES, SEQ, D)
    normed_one = (normalize(residual) * (1.0 + mod_terms[:, 1]) + mod_terms[:, 0]).astype(jnp.bfloat16).reshape(TOKENS, D)
    query_rows = jnp.dot(normed_one, w_query, preferred_element_type=jnp.float32).astype(jnp.bfloat16)
    key_rows = jnp.dot(normed_one, w_key, preferred_element_type=jnp.float32).astype(jnp.bfloat16)
    value_rows = jnp.dot(normed_one, w_value, preferred_element_type=jnp.float32).astype(jnp.bfloat16)
    query_four = query_rows.astype(jnp.float32).reshape(IMAGES, SEQ, HEADS, HDIM)
    key_four = key_rows.astype(jnp.float32).reshape(IMAGES, SEQ, HEADS, HDIM)
    value_four = value_rows.astype(jnp.float32).reshape(IMAGES, SEQ, HEADS, HDIM)
    scores = jnp.einsum('bqhd,bkhd->bhqk', query_four, key_four) * HDIM ** (-0.5)
    row_peak = lax.optimization_barrier(jnp.max(scores, axis=-1, keepdims=True))
    exponent = jnp.exp(scores - row_peak)
    attn_weights = (exponent / lax.optimization_barrier(jnp.sum(exponent, axis=-1, keepdims=True))).astype(jnp.bfloat16)
    mixed_heads = jnp.einsum('bhqk,bkhd->bqhd', attn_weights.astype(jnp.float32), value_four)
    mixed_heads = mixed_heads.astype(jnp.bfloat16).reshape(TOKENS, HW)
    projected = jnp.dot(mixed_heads, w_out, preferred_element_type=jnp.float32).reshape(IMAGES, SEQ, D)
    after_attn = residual + mod_terms[:, 2] * projected
    normed_two = (normalize(after_attn) * (1.0 + mod_terms[:, 4]) + mod_terms[:, 3]).astype(jnp.bfloat16)
    normed_two = normed_two.reshape(devices, TOK_DEV, D)
    slots = jax.vmap(slot_table)(routes.reshape(devices, TOK_DEV * TOP))
    token_of = jnp.arange(TOK_DEV * TOP, dtype=jnp.int32) // TOP

    def fill_slots(source_rows, where):
        return jnp.zeros((E * CAP, D), jnp.bfloat16).at[where].set(source_rows[token_of])
    buffers = jax.vmap(fill_slots)(normed_two, slots)
    per_expert = buffers.reshape(devices, E, CAP, D).transpose(1, 0, 2, 3).reshape(E, devices * CAP, D)

    def expert_pass(operands):
        expert_rows, w_first, w_second = operands
        hidden = jax.nn.gelu(jnp.dot(expert_rows, w_first, preferred_element_type=jnp.float32), approximate=True)
        hidden = hidden.astype(jnp.bfloat16)
        return jnp.dot(hidden, w_second, preferred_element_type=jnp.float32).astype(jnp.bfloat16)
    outputs = lax.map(expert_pass, (per_expert, w_in, w_back))
    returned = outputs.reshape(E, devices, CAP, D).transpose(1, 0, 2, 3).reshape(devices, E * CAP, D)
    picked = jax.vmap(lambda table, where: table[where])(returned, slots)
    picked = picked.astype(jnp.float32).reshape(TOKENS, TOP, D)
    expert_mix = lax.optimization_barrier(jnp.sum(route_prob[:, :, None] * picked, axis=1)).reshape(IMAGES, SEQ, D)
    return (after_attn + mod_terms[:, 5] * expert_mix).astype(jnp.bfloat16).reshape(TOKENS, D)
```

```python
import functools

import jax
import jax.numpy as jnp
from jax import lax
from jax.experimental import pallas as pl
from jax.experimental.pallas import tpu as pltpu
from jax.sharding import PartitionSpec as P

HEADS = 8
HDIM = 128
TOP = 2


def normalize(values):
    row_mean = jnp.mean(values, axis=-1, keepdims=True)
    centered = values - row_mean
    variance = jnp.mean(centered * centered, axis=-1, keepdims=True)
    return centered * lax.rsqrt(variance + 1e-06)


MESH = pl.DeviceIdType.MESH
ORDERS = ((0, 2, 1), (0, 1, 2), (2, 0, 1), (1, 0, 2))


def axis_sizes(count):
    sizes = [1, 1, 1]
    at = 0
    while count > 1:
        factor = next(f for f in range(2, count + 1) if count % f == 0)
        sizes[at % 3] *= factor
        count //= factor
        at += 1
    return tuple(sizes)


def gather_kernel(sizes, *refs):
    blocks, outs = refs[:4], refs[4:8]
    own_sem, send_sem, recv_sem, side_send, side_recv = refs[8:]
    grp = lax.axis_index("grp")
    dev = lax.axis_index("dev")
    other = 1 - grp
    coords = (dev // (sizes[1] * sizes[2]), (dev // sizes[2]) % sizes[1], dev % sizes[2])

    def peer(axis, offset):
        moved = list(coords)
        moved[axis] = (coords[axis] + offset) % sizes[axis]
        return (moved[0] * sizes[1] + moved[1]) * sizes[2] + moved[2], moved[axis]

    barrier = pltpu.get_barrier_semaphore()
    greeted = 1
    pl.semaphore_signal(barrier, inc=1, device_id=(other, dev), device_id_type=MESH)
    for axis in range(3):
        for offset in range(1, sizes[axis]):
            pl.semaphore_signal(
                barrier, inc=1, device_id=(grp, peer(axis, offset)[0]), device_id_type=MESH
            )
            greeted += 1
    pl.semaphore_wait(barrier, greeted)

    slot_of = [[None] * 3 for _ in range(4)]
    for chunk in range(4):
        used = 0
        for stage in range(3):
            slot_of[chunk][stage] = used
            used += sizes[ORDERS[chunk][stage]] - 1

    def region(chunk, half, stage, coordinate):
        where = [half]
        for axis in range(3):
            place = ORDERS[chunk].index(axis)
            if place < stage:
                where.append(slice(None))
            elif place == stage:
                where.append(coordinate)
            else:
                where.append(coords[axis])
        return outs[chunk].at[tuple(where)]

    def link_copy(chunk, stage, offset, source, target):
        axis = ORDERS[chunk][stage]
        slot = slot_of[chunk][stage] + offset - 1
        return pltpu.make_async_remote_copy(
            src_ref=source,
            dst_ref=target,
            send_sem=send_sem.at[chunk, slot],
            recv_sem=recv_sem.at[chunk, slot],
            device_id=(grp, peer(axis, offset)[0]),
            device_id_type=MESH,
        )

    def side_copy(chunk, slot, source, target):
        return pltpu.make_async_remote_copy(
            src_ref=source,
            dst_ref=target,
            send_sem=side_send.at[chunk, slot],
            recv_sem=side_recv.at[chunk, slot],
            device_id=(other, dev),
            device_id_type=MESH,
        )

    pending = []

    def start_stage(chunk, stage):
        axis = ORDERS[chunk][stage]
        mine = region(chunk, grp, stage, coords[axis])
        source = blocks[chunk] if stage == 0 else mine
        for offset in range(1, sizes[axis]):
            copy = link_copy(chunk, stage, offset, source, mine)
            copy.start()
            pending.append(copy)

    def finish_stage(chunk, stage):
        axis = ORDERS[chunk][stage]
        for offset in range(1, sizes[axis]):
            came = peer(axis, sizes[axis] - offset)[1]
            landed = region(chunk, grp, stage, came)
            link_copy(chunk, stage, offset, landed, landed).wait_recv()

    def pass_on(chunk, stage):
        axis = ORDERS[chunk][stage]
        for offset in range(1, sizes[axis]):
            came = peer(axis, sizes[axis] - offset)[1]
            slot = slot_of[chunk][stage] + offset
            landed = region(chunk, grp, stage, came)
            copy = side_copy(chunk, slot, landed, landed)
            copy.start()
            pending.append(copy)
            theirs = region(chunk, other, stage, came)
            arriving.append(side_copy(chunk, slot, theirs, theirs))

    arriving = []
    own = []
    for chunk in (0, 2, 3, 1):
        start_stage(chunk, 0)
    for chunk in range(4):
        place = region(chunk, grp, 0, coords[ORDERS[chunk][0]])
        copy = pltpu.make_async_copy(blocks[chunk], place, own_sem.at[chunk])
        copy.start()
        own.append(copy)
        copy = side_copy(chunk, 0, blocks[chunk], place)
        copy.start()
        pending.append(copy)
        theirs = region(chunk, other, 0, coords[ORDERS[chunk][0]])
        arriving.append(side_copy(chunk, 0, theirs, theirs))
    for copy in own:
        copy.wait()
    for stage in range(3):
        for chunk in (2, 3, 0, 1) if stage == 0 else (0, 1, 2, 3):
            finish_stage(chunk, stage)
            if stage < 2:
                start_stage(chunk, stage + 1)
            pass_on(chunk, stage)
    for copy in arriving:
        copy.wait_recv()
    for copy in pending:
        copy.wait_send()


def gather_weights(*blocks):
    n_grp, n_dev = lax.axis_size("grp"), lax.axis_size("dev")
    sizes = axis_sizes(n_dev)
    peers = sum(sizes) - 3
    full = jax.ShapeDtypeStruct((n_grp,) + sizes + blocks[0].shape, blocks[0].dtype)
    gathered = pl.pallas_call(
        functools.partial(gather_kernel, sizes),
        out_shape=[full] * 4,
        in_specs=[pl.BlockSpec(memory_space=pltpu.VMEM)] * 4,
        out_specs=[pl.BlockSpec(memory_space=pl.ANY)] * 4,
        scratch_shapes=[
            pltpu.SemaphoreType.DMA((4,)),
            pltpu.SemaphoreType.DMA((4, peers)),
            pltpu.SemaphoreType.DMA((4, peers)),
            pltpu.SemaphoreType.DMA((4, peers + 1)),
            pltpu.SemaphoreType.DMA((4, peers + 1)),
        ],
        compiler_params=pltpu.CompilerParams(collective_id=0, has_side_effects=True),
    )(*blocks)
    return [whole.reshape(-1, blocks[0].shape[1]) for whole in gathered]


def add_columns(normed, weight_rows):
    return jnp.dot(normed, weight_rows, preferred_element_type=jnp.float32)


def expert_half(stacked, w_first, w_second):
    grouped = stacked.reshape(-1, w_first.shape[0], stacked.shape[1], stacked.shape[2])
    hidden = jnp.einsum("secd,edf->secf", grouped, w_first, preferred_element_type=jnp.float32)
    hidden = jax.nn.gelu(hidden, approximate=True).astype(jnp.bfloat16)
    partial_out = jnp.einsum("secf,efd->secd", hidden, w_second, preferred_element_type=jnp.float32)
    return partial_out.reshape(stacked.shape)


def body(tokens, modulation, w_query, w_key, w_value, w_out, w_in, w_back, routes, route_prob):
    tok_rows, width = tokens.shape
    all_query, all_key, all_value, all_out = gather_weights(w_query, w_key, w_value, w_out.T)
    images = modulation.shape[0]
    seq_len = tok_rows // images
    mod_terms = modulation.reshape(images, 6, 1, width)
    residual = tokens.astype(jnp.float32).reshape(images, seq_len, width)
    normed_one = (normalize(residual) * (1.0 + mod_terms[:, 1]) + mod_terms[:, 0]).astype(
        jnp.bfloat16
    )
    normed_one = normed_one.reshape(tok_rows, width)
    inner = w_query.shape[1]

    def add_one(weight_rows):
        return add_columns(normed_one, weight_rows)

    query_rows = add_one(all_query)
    key_rows = add_one(all_key)
    value_rows = add_one(all_value)
    query_four = query_rows.astype(jnp.bfloat16).reshape(images, seq_len, HEADS, HDIM)
    key_four = key_rows.astype(jnp.bfloat16).reshape(images, seq_len, HEADS, HDIM)
    value_four = value_rows.astype(jnp.bfloat16).reshape(images, seq_len, HEADS, HDIM)
    scores = jnp.einsum(
        "bqhd,bkhd->bhqk", query_four, key_four, preferred_element_type=jnp.float32
    ) * HDIM ** (-0.5)
    row_peak = jnp.max(scores, axis=-1, keepdims=True)
    exponent = jnp.exp(scores - row_peak)
    attn_weights = (exponent / jnp.sum(exponent, axis=-1, keepdims=True)).astype(jnp.bfloat16)
    mixed_heads = jnp.einsum(
        "bhqk,bkhd->bqhd", attn_weights, value_four, preferred_element_type=jnp.float32
    )
    mixed_heads = mixed_heads.astype(jnp.bfloat16).reshape(tok_rows, inner)
    projected = lax.dot_general(
        mixed_heads,
        all_out,
        (((1,), (1,)), ((), ())),
        preferred_element_type=jnp.float32,
    ).reshape(images, seq_len, width)
    after_attn = residual + mod_terms[:, 2] * projected
    normed_two = (normalize(after_attn) * (1.0 + mod_terms[:, 4]) + mod_terms[:, 3]).astype(
        jnp.bfloat16
    )
    normed_two = normed_two.reshape(tok_rows, width)
    local_experts = w_in.shape[0]
    experts = local_experts * lax.axis_size("dev")
    capacity = max(2, tok_rows * TOP * 5 // (experts * 4))
    choice_ids = routes.reshape(-1)
    onehot = (choice_ids[:, None] == jnp.arange(experts, dtype=jnp.int32)[None, :]).astype(
        jnp.int32
    )
    before = jnp.cumsum(onehot, axis=0) - onehot
    slots = choice_ids * capacity + jnp.sum(before * onehot, axis=1)
    slots = slots.reshape(tok_rows, TOP)
    places = jnp.arange(experts * capacity, dtype=jnp.int32)
    chosen = slots[:, :, None] == places[None, None, :]
    outgoing = lax.dot_general(
        jnp.any(chosen, axis=1).astype(jnp.bfloat16),
        normed_two,
        (((0,), (0,)), ((), ())),
        preferred_element_type=jnp.float32,
    ).astype(jnp.bfloat16)
    outgoing = outgoing.reshape(experts, capacity, width)
    arrived = lax.all_to_all(outgoing, "dev", split_axis=0, concat_axis=0, tiled=True)
    fanned = lax.all_gather(arrived, "grp", axis=0, tiled=True)
    summed = lax.psum_scatter(
        expert_half(fanned, w_in, w_back).astype(jnp.bfloat16),
        "grp",
        scatter_dimension=0,
        tiled=True,
    )
    back_rows = lax.all_to_all(summed, "dev", split_axis=0, concat_axis=0, tiled=True)
    back_rows = back_rows.reshape(experts * capacity, width)
    expert_mix = 0.0
    for choice in range(TOP):
        picked = jnp.dot(
            chosen[:, choice].astype(jnp.bfloat16), back_rows, preferred_element_type=jnp.float32
        )
        expert_mix = expert_mix + route_prob[:, choice, None] * picked
    expert_mix = expert_mix.reshape(images, seq_len, width)
    return (after_attn + mod_terms[:, 5] * expert_mix).astype(jnp.bfloat16).reshape(tok_rows, width)


def solution(mesh):
    in_specs = (
        P(("grp", "dev"), None),
        P(("grp", "dev"), None),
        P(("grp", "dev"), None),
        P(("grp", "dev"), None),
        P(("grp", "dev"), None),
        P(None, ("grp", "dev")),
        P("dev", None, "grp"),
        P("dev", "grp", None),
        P(("grp", "dev"), None),
        P(("grp", "dev"), None),
    )
    out_specs = P(("grp", "dev"), None)
    return jax.shard_map(body, mesh=mesh, in_specs=in_specs, out_specs=out_specs, check_vma=False)
```

```python
import functools

import jax
import jax.numpy as jnp
from jax import lax
from jax.experimental import pallas as pl
from jax.experimental.pallas import tpu as pltpu
from jax.sharding import PartitionSpec as P

HEADS = 8
HDIM = 128
TOP = 2


def normalize(values):
    row_mean = jnp.mean(values, axis=-1, keepdims=True)
    centered = values - row_mean
    variance = jnp.mean(centered * centered, axis=-1, keepdims=True)
    return centered * lax.rsqrt(variance + 1e-06)


MESH = pl.DeviceIdType.MESH
ORDERS = ((0, 2, 1), (0, 1, 2), (2, 0, 1), (1, 0, 2))


def axis_sizes(count):
    sizes = [1, 1, 1]
    at = 0
    while count > 1:
        factor = next(f for f in range(2, count + 1) if count % f == 0)
        sizes[at % 3] *= factor
        count //= factor
        at += 1
    return tuple(sizes)


def gather_kernel(sizes, *refs):
    blocks, outs = refs[:4], refs[4:8]
    own_sem, send_sem, recv_sem, side_send, side_recv = refs[8:]
    grp = lax.axis_index("grp")
    dev = lax.axis_index("dev")
    other = 1 - grp
    coords = (dev // (sizes[1] * sizes[2]), (dev // sizes[2]) % sizes[1], dev % sizes[2])

    def peer(axis, offset):
        moved = list(coords)
        moved[axis] = (coords[axis] + offset) % sizes[axis]
        return (moved[0] * sizes[1] + moved[1]) * sizes[2] + moved[2], moved[axis]

    barrier = pltpu.get_barrier_semaphore()
    greeted = 1
    pl.semaphore_signal(barrier, inc=1, device_id=(other, dev), device_id_type=MESH)
    for axis in range(3):
        for offset in range(1, sizes[axis]):
            pl.semaphore_signal(
                barrier, inc=1, device_id=(grp, peer(axis, offset)[0]), device_id_type=MESH
            )
            greeted += 1
    pl.semaphore_wait(barrier, greeted)

    slot_of = [[None] * 3 for _ in range(4)]
    for chunk in range(4):
        used = 0
        for stage in range(3):
            slot_of[chunk][stage] = used
            used += sizes[ORDERS[chunk][stage]] - 1

    def region(chunk, half, stage, coordinate):
        where = [half]
        for axis in range(3):
            place = ORDERS[chunk].index(axis)
            if place < stage:
                where.append(slice(None))
            elif place == stage:
                where.append(coordinate)
            else:
                where.append(coords[axis])
        return outs[chunk].at[tuple(where)]

    def link_copy(chunk, stage, offset, source, target):
        axis = ORDERS[chunk][stage]
        slot = slot_of[chunk][stage] + offset - 1
        return pltpu.make_async_remote_copy(
            src_ref=source,
            dst_ref=target,
            send_sem=send_sem.at[chunk, slot],
            recv_sem=recv_sem.at[chunk, slot],
            device_id=(grp, peer(axis, offset)[0]),
            device_id_type=MESH,
        )

    def side_copy(chunk, slot, source, target):
        return pltpu.make_async_remote_copy(
            src_ref=source,
            dst_ref=target,
            send_sem=side_send.at[chunk, slot],
            recv_sem=side_recv.at[chunk, slot],
            device_id=(other, dev),
            device_id_type=MESH,
        )

    pending = []

    def start_stage(chunk, stage):
        axis = ORDERS[chunk][stage]
        mine = region(chunk, grp, stage, coords[axis])
        source = blocks[chunk] if stage == 0 else mine
        for offset in range(1, sizes[axis]):
            copy = link_copy(chunk, stage, offset, source, mine)
            copy.start()
            pending.append(copy)

    def finish_stage(chunk, stage):
        axis = ORDERS[chunk][stage]
        for offset in range(1, sizes[axis]):
            came = peer(axis, sizes[axis] - offset)[1]
            landed = region(chunk, grp, stage, came)
            link_copy(chunk, stage, offset, landed, landed).wait_recv()

    def pass_on(chunk, stage):
        axis = ORDERS[chunk][stage]
        for offset in range(1, sizes[axis]):
            came = peer(axis, sizes[axis] - offset)[1]
            slot = slot_of[chunk][stage] + offset
            landed = region(chunk, grp, stage, came)
            copy = side_copy(chunk, slot, landed, landed)
            copy.start()
            pending.append(copy)
            theirs = region(chunk, other, stage, came)
            arriving.append(side_copy(chunk, slot, theirs, theirs))

    arriving = []
    own = []
    for chunk in (0, 2, 3, 1):
        start_stage(chunk, 0)
    for chunk in range(4):
        place = region(chunk, grp, 0, coords[ORDERS[chunk][0]])
        copy = pltpu.make_async_copy(blocks[chunk], place, own_sem.at[chunk])
        copy.start()
        own.append(copy)
        copy = side_copy(chunk, 0, blocks[chunk], place)
        copy.start()
        pending.append(copy)
        theirs = region(chunk, other, 0, coords[ORDERS[chunk][0]])
        arriving.append(side_copy(chunk, 0, theirs, theirs))
    for copy in own:
        copy.wait()
    for stage in range(3):
        for chunk in (2, 3, 0, 1) if stage == 0 else (0, 1, 2, 3):
            finish_stage(chunk, stage)
            if stage < 2:
                start_stage(chunk, stage + 1)
            pass_on(chunk, stage)
    for copy in arriving:
        copy.wait_recv()
    for copy in pending:
        copy.wait_send()


def gather_weights(*blocks):
    n_grp, n_dev = lax.axis_size("grp"), lax.axis_size("dev")
    sizes = axis_sizes(n_dev)
    peers = sum(sizes) - 3
    full = jax.ShapeDtypeStruct((n_grp,) + sizes + blocks[0].shape, blocks[0].dtype)
    gathered = pl.pallas_call(
        functools.partial(gather_kernel, sizes),
        out_shape=[full] * 4,
        in_specs=[pl.BlockSpec(memory_space=pltpu.VMEM)] * 4,
        out_specs=[pl.BlockSpec(memory_space=pl.ANY)] * 4,
        scratch_shapes=[
            pltpu.SemaphoreType.DMA((4,)),
            pltpu.SemaphoreType.DMA((4, peers)),
            pltpu.SemaphoreType.DMA((4, peers)),
            pltpu.SemaphoreType.DMA((4, peers + 1)),
            pltpu.SemaphoreType.DMA((4, peers + 1)),
        ],
        compiler_params=pltpu.CompilerParams(collective_id=0, has_side_effects=True),
    )(*blocks)
    return [whole.reshape(-1, blocks[0].shape[1]) for whole in gathered]


def add_columns(normed, weight_rows):
    return jnp.dot(normed, weight_rows, preferred_element_type=jnp.float32)


TILE = 512


def expert_kernel(
    sizes, outgoing, first_hbm, second_hbm, back, arrived, give, got, summed, first, second,
    wide, rows, hidden, own, theirs,
    weight_sem, local_sem, out_send, out_recv, fan_send, fan_recv, swap_send, swap_recv,
    back_send, back_recv,
):
    grp = lax.axis_index("grp")
    dev = lax.axis_index("dev")
    other = 1 - grp
    plane = sizes[1] * sizes[2]
    count = sizes[0] * plane
    cap, width = outgoing.shape[1], outgoing.shape[2]
    depth = dev // plane
    high = (dev // sizes[2]) % sizes[1]
    low = dev % sizes[2]

    def shifted(slot, sign):
        a = (depth + sign * (slot // plane) + sizes[0]) % sizes[0]
        b = (high + sign * ((slot // sizes[2]) % sizes[1]) + sizes[1]) % sizes[1]
        c = (low + sign * (slot % sizes[2]) + sizes[2]) % sizes[2]
        return (a * sizes[1] + b) * sizes[2] + c

    def remote(source, target, send_sem, recv_sem, device):
        return pltpu.make_async_remote_copy(
            src_ref=source,
            dst_ref=target,
            send_sem=send_sem,
            recv_sem=recv_sem,
            device_id=device,
            device_id_type=MESH,
        )

    def dispatch(slot):
        owner = shifted(slot, 1)
        return remote(
            outgoing.at[owner], arrived.at[0, slot], out_send.at[slot], out_recv.at[slot],
            (grp, owner),
        )

    def fan(slot):
        return remote(
            arrived.at[0, slot], arrived.at[1, slot], fan_send.at[slot], fan_recv.at[slot],
            (other, dev),
        )

    def swap(group):
        part = pl.ds(group * plane, plane)
        return remote(
            give.at[part], got.at[part], swap_send.at[group], swap_recv.at[group], (other, dev)
        )

    def give_back(slot):
        return remote(
            summed.at[slot], back.at[dev], back_send.at[slot], back_recv.at[slot],
            (grp, shifted(slot, -1)),
        )

    def come_back(slot):
        owner = shifted(slot, 1)
        return remote(
            summed.at[slot], back.at[owner], back_send.at[slot], back_recv.at[slot], (grp, owner)
        )

    barrier = pltpu.get_barrier_semaphore()
    pl.semaphore_signal(barrier, inc=1, device_id=(other, dev), device_id_type=MESH)
    for slot in range(1, count):
        pl.semaphore_signal(
            barrier, inc=1, device_id=(grp, shifted(slot, 1)), device_id_type=MESH
        )
    pl.semaphore_wait(barrier, count)

    for slot in range(1, count):
        dispatch(slot).start()
    stay = pltpu.make_async_copy(outgoing.at[dev], arrived.at[0, 0], local_sem.at[0])
    stay.start()
    load_first = pltpu.make_async_copy(first_hbm.at[0], first, weight_sem.at[0])
    load_second = pltpu.make_async_copy(second_hbm.at[0], second, weight_sem.at[1])
    load_first.start()
    load_second.start()
    stay.wait()
    fan(0).start()
    load_first.wait()
    load_second.wait()

    def tiles(total):
        return total // TILE

    def columns(at):
        return pl.ds(pl.multiple_of(at * TILE, TILE), TILE)

    def slab(at):
        return pl.ds(pl.multiple_of(at * cap, 8), cap)

    def one_group(group, carry):
        def pass_on(place, carry):
            slot = group * plane + place

            @pl.when(slot > 0)
            def _():
                dispatch(slot).wait_recv()
                fan(slot).start()

            return carry

        lax.fori_loop(0, plane, pass_on, 0)

        def spread(place, carry):
            slot = group * plane + place
            fan(slot).wait_recv()
            wide[slab(place), :] = arrived[0, slot].astype(jnp.float32)
            wide[slab(plane + place), :] = arrived[1, slot].astype(jnp.float32)
            return carry

        lax.fori_loop(0, plane, spread, 0)

        def narrow(at, carry):
            rows[:, columns(at)] = wide[:, columns(at)].astype(jnp.bfloat16)
            return carry

        lax.fori_loop(0, tiles(width), narrow, 0)

        def up(at, carry):
            raised = jnp.dot(
                rows[...], first[:, columns(at)], preferred_element_type=jnp.float32
            )
            hidden[:, columns(at)] = jax.nn.gelu(raised, approximate=True).astype(jnp.bfloat16)
            return carry

        lax.fori_loop(0, tiles(first.shape[1]), up, 0)

        def down(at, carry):
            lowered = jnp.dot(
                hidden[...], second[:, columns(at)], preferred_element_type=jnp.float32
            )
            own[:, columns(at)] = lowered[: plane * cap]
            theirs[:, columns(at)] = lowered[plane * cap :]
            return carry

        lax.fori_loop(0, tiles(width), down, 0)

        def pack(place, carry):
            give[group * plane + place] = theirs[slab(place), :].astype(jnp.bfloat16)
            return carry

        lax.fori_loop(0, plane, pack, 0)
        swap(group).start()
        swap(group).wait_recv()

        def total(place, carry):
            slot = group * plane + place
            summed[slot] = (own[slab(place), :] + got[slot].astype(jnp.float32)).astype(
                jnp.bfloat16
            )

            @pl.when(slot > 0)
            def _():
                give_back(slot).start()

            return carry

        lax.fori_loop(0, plane, total, 0)
        return carry

    lax.fori_loop(0, sizes[0], one_group, 0)
    keep = pltpu.make_async_copy(summed.at[0], back.at[dev], local_sem.at[0])
    keep.start()
    keep.wait()
    for slot in range(1, count):
        dispatch(slot).wait_send()
        come_back(slot).wait_recv()
        give_back(slot).wait_send()
    for slot in range(count):
        fan(slot).wait_send()
    for group in range(sizes[0]):
        swap(group).wait_send()


def run_experts(outgoing, w_in, w_back):
    sizes = axis_sizes(lax.axis_size("dev"))
    count, cap, width = outgoing.shape
    plane = sizes[1] * sizes[2]
    many = 2 * plane * cap
    bf16, f32 = jnp.bfloat16, jnp.float32
    dma = pltpu.SemaphoreType.DMA
    anywhere = pl.BlockSpec(memory_space=pl.ANY)
    return pl.pallas_call(
        functools.partial(expert_kernel, sizes),
        out_shape=jax.ShapeDtypeStruct(outgoing.shape, bf16),
        in_specs=[pl.BlockSpec(memory_space=pltpu.VMEM), anywhere, anywhere],
        out_specs=anywhere,
        scratch_shapes=[
            pltpu.VMEM((2, count, cap, width), bf16),
            pltpu.VMEM((count, cap, width), bf16),
            pltpu.VMEM((count, cap, width), bf16),
            pltpu.VMEM((count, cap, width), bf16),
            pltpu.VMEM(w_in.shape[1:], bf16),
            pltpu.VMEM(w_back.shape[1:], bf16),
            pltpu.VMEM((many, width), f32),
            pltpu.VMEM((many, width), bf16),
            pltpu.VMEM((many, w_in.shape[2]), bf16),
            pltpu.VMEM((plane * cap, width), f32),
            pltpu.VMEM((plane * cap, width), f32),
            dma((2,)),
            dma((1,)),
            dma((count,)),
            dma((count,)),
            dma((count,)),
            dma((count,)),
            dma((sizes[0],)),
            dma((sizes[0],)),
            dma((count,)),
            dma((count,)),
        ],
        compiler_params=pltpu.CompilerParams(
            collective_id=1, has_side_effects=True, vmem_limit_bytes=63 * 1024 * 1024
        ),
    )(outgoing, w_in, w_back)


def body(tokens, modulation, w_query, w_key, w_value, w_out, w_in, w_back, routes, route_prob):
    tok_rows, width = tokens.shape
    all_query, all_key, all_value, all_out = gather_weights(w_query, w_key, w_value, w_out.T)
    images = modulation.shape[0]
    seq_len = tok_rows // images
    mod_terms = modulation.reshape(images, 6, 1, width)
    residual = tokens.astype(jnp.float32).reshape(images, seq_len, width)
    normed_one = (normalize(residual) * (1.0 + mod_terms[:, 1]) + mod_terms[:, 0]).astype(
        jnp.bfloat16
    )
    normed_one = normed_one.reshape(tok_rows, width)
    inner = w_query.shape[1]

    def add_one(weight_rows):
        return add_columns(normed_one, weight_rows)

    query_rows = add_one(all_query)
    key_rows = add_one(all_key)
    value_rows = add_one(all_value)
    query_four = query_rows.astype(jnp.bfloat16).reshape(images, seq_len, HEADS, HDIM)
    key_four = key_rows.astype(jnp.bfloat16).reshape(images, seq_len, HEADS, HDIM)
    value_four = value_rows.astype(jnp.bfloat16).reshape(images, seq_len, HEADS, HDIM)
    scores = jnp.einsum(
        "bqhd,bkhd->bhqk", query_four, key_four, preferred_element_type=jnp.float32
    ) * HDIM ** (-0.5)
    row_peak = jnp.max(scores, axis=-1, keepdims=True)
    exponent = jnp.exp(scores - row_peak)
    attn_weights = (exponent / jnp.sum(exponent, axis=-1, keepdims=True)).astype(jnp.bfloat16)
    mixed_heads = jnp.einsum(
        "bhqk,bkhd->bqhd", attn_weights, value_four, preferred_element_type=jnp.float32
    )
    mixed_heads = mixed_heads.astype(jnp.bfloat16).reshape(tok_rows, inner)
    projected = lax.dot_general(
        mixed_heads,
        all_out,
        (((1,), (1,)), ((), ())),
        preferred_element_type=jnp.float32,
    ).reshape(images, seq_len, width)
    after_attn = residual + mod_terms[:, 2] * projected
    normed_two = (normalize(after_attn) * (1.0 + mod_terms[:, 4]) + mod_terms[:, 3]).astype(
        jnp.bfloat16
    )
    normed_two = normed_two.reshape(tok_rows, width)
    local_experts = w_in.shape[0]
    experts = local_experts * lax.axis_size("dev")
    capacity = max(2, tok_rows * TOP * 5 // (experts * 4))
    capacity = -(-capacity // 8) * 8
    choice_ids = routes.reshape(-1)
    onehot = (choice_ids[:, None] == jnp.arange(experts, dtype=jnp.int32)[None, :]).astype(
        jnp.int32
    )
    before = jnp.cumsum(onehot, axis=0) - onehot
    slots = choice_ids * capacity + jnp.sum(before * onehot, axis=1)
    slots = slots.reshape(tok_rows, TOP)
    places = jnp.arange(experts * capacity, dtype=jnp.int32)
    chosen = slots[:, :, None] == places[None, None, :]
    outgoing = lax.dot_general(
        jnp.any(chosen, axis=1).astype(jnp.bfloat16),
        normed_two,
        (((0,), (0,)), ((), ())),
        preferred_element_type=jnp.float32,
    ).astype(jnp.bfloat16)
    outgoing = outgoing.reshape(experts, capacity, width)
    back_rows = run_experts(outgoing, w_in, w_back)
    back_rows = back_rows.reshape(experts * capacity, width)
    expert_mix = 0.0
    for choice in range(TOP):
        picked = jnp.dot(
            chosen[:, choice].astype(jnp.bfloat16), back_rows, preferred_element_type=jnp.float32
        )
        expert_mix = expert_mix + route_prob[:, choice, None] * picked
    expert_mix = expert_mix.reshape(images, seq_len, width)
    return (after_attn + mod_terms[:, 5] * expert_mix).astype(jnp.bfloat16).reshape(tok_rows, width)


def solution(mesh):
    in_specs = (
        P(("grp", "dev"), None),
        P(("grp", "dev"), None),
        P(("grp", "dev"), None),
        P(("grp", "dev"), None),
        P(("grp", "dev"), None),
        P(None, ("grp", "dev")),
        P("dev", None, "grp"),
        P("dev", "grp", None),
        P(("grp", "dev"), None),
        P(("grp", "dev"), None),
    )
    out_specs = P(("grp", "dev"), None)
    return jax.shard_map(body, mesh=mesh, in_specs=in_specs, out_specs=out_specs, check_vma=False)
```
